128 devices in a mesh: blk: 64 (over x_lo, y, z, core), grp: 2 (over x_hi).
Axes of the slice: x: 4 (x_hi: 2, x_lo: 2; x = x_hi * 2 + x_lo), y: 4, z: 4, core: 2. Of those that a mesh axis runs over, the one named last changes fastest.
Arguments:
- star_state: float32 [13, 32768], P(None, 'blk')
- active_local: int32 [8192], P(('blk', 'grp')), may hold values from 0 to 511, as said below
- neighbours: int32 [8192, 64], P(('blk', 'grp')), may hold values from 0 to 32767, as said below
- counts: int32 [8192], P(('blk', 'grp')), may hold values from 1 to 64, as said below
Outputs:
- new_state: float32 [6, 8192], P(None, ('blk', 'grp'))
- regular: float32 [6, 8192], P(None, ('blk', 'grp'))
- irregular: float32 [6, 8192], P(None, ('blk', 'grp'))
The draws below stay inside these ranges and needn't reach their ends.
Inputs may be any that keep to these rules, and one draw needn't show every extreme that they name: `active_local`: distinct within one blk index over its grp devices. Some device's actives all have counts 64. `neighbours`: over one device's live entries (k < counts), each blk index owns (id // 512) at most 64 of them, reached on some device; entries at k >= counts name the active itself.
All inputs are finite; a program needn't handle non-finite values.
Results may differ from the reference program's by a relative error of at most 0.00002.
Values sent between devices are 32-bit elements; how exact they have to be, the bound alone decides.
No kernel may reach another device: no remote copies, remote signals or barrier semaphores. Data moves between devices by JAX's collectives and lax.ppermute only.
A program may use at most 128 MiB of HBM per device.

```python
import math
import jax
import jax.numpy as jnp
from jax import lax

FIELD_DEV = 512
A_DEV = 64
NB = 64
CLSZ = 16
STARS = 32768
ACTIVES = 8192
N_BLK = 64
N_GRP = 2


def coarse_layout(key):
    layout_key = jax.random.fold_in(key, 303)
    coarse_cell = jax.vmap(lambda subkey: jax.random.permutation(subkey, FIELD_DEV))(jax.random.split(layout_key, N_BLK)).astype(jnp.int32)
    shard_rows = jnp.broadcast_to(jnp.arange(N_BLK, dtype=jnp.int32)[:, None], (N_BLK, FIELD_DEV))
    field_values = jnp.broadcast_to(jnp.arange(FIELD_DEV, dtype=jnp.int32)[None, :], (N_BLK, FIELD_DEV))
    field_at = jnp.zeros((N_BLK, FIELD_DEV), jnp.int32).at[shard_rows, coarse_cell].set(field_values)
    return (coarse_cell, field_at)


def integer_parts(key):
    base_key = jax.random.fold_in(key, 101)
    subkeys = jax.random.split(base_key, 6)
    devices = N_BLK * N_GRP
    coarse_cell, field_at = coarse_layout(key)
    shard_perms = jax.vmap(lambda subkey: jax.random.permutation(subkey, FIELD_DEV))(jax.random.split(subkeys[0], N_BLK))
    active_local = shard_perms[:, :N_GRP * A_DEV].reshape(devices, A_DEV).astype(jnp.int32)
    upper_count = jax.random.randint(subkeys[1], (devices,), NB // 2, NB + 1)
    full_device = jax.random.randint(subkeys[2], (), 0, devices)
    marker = jnp.arange(devices) == full_device
    upper_count = jnp.where(marker, NB, upper_count)
    lower_count = jnp.where(marker, NB, jnp.maximum(1, upper_count // 2))
    random_bits = jax.random.randint(subkeys[3], (devices, A_DEV), 0, 1 << 20)
    counts = lower_count[:, None] + random_bits % (upper_count - lower_count + 1)[:, None]
    live_mask = jnp.arange(NB)[None, None, :] < counts[:, :, None]
    live_order = jnp.cumsum(live_mask.reshape(devices, A_DEV * NB).astype(jnp.int32), axis=1) - 1
    owner_perm = jax.vmap(lambda subkey: jax.random.permutation(subkey, N_BLK))(jax.random.split(subkeys[4], devices))
    owner_blk = jnp.take_along_axis(owner_perm, jnp.maximum(live_order, 0) % N_BLK, axis=1).reshape(devices, A_DEV, NB).astype(jnp.int32)
    home_shard = jnp.arange(devices, dtype=jnp.int32) // N_GRP
    home_blk = home_shard[:, None, None]
    home_cells = jnp.take_along_axis(coarse_cell[home_shard], active_local, axis=1)
    member = jax.random.randint(subkeys[5], (devices, A_DEV, NB), 0, CLSZ)
    target_cell = (home_cells // CLSZ)[:, :, None] * CLSZ + member
    near_field = field_at[owner_blk, target_cell]
    near_ids = owner_blk * FIELD_DEV + near_field
    itself = home_blk * FIELD_DEV + active_local[:, :, None]
    neighbours = jnp.where(live_mask, near_ids, itself)
    return (active_local.reshape(-1).astype(jnp.int32), neighbours.reshape(devices * A_DEV, NB).astype(jnp.int32), counts.reshape(-1).astype(jnp.int32))


def draw_active_local(key, part):
    return integer_parts(key)[0]


def draw_neighbours(key, part):
    return integer_parts(key)[1]


def draw_counts(key, part):
    return integer_parts(key)[2]


def lattice_cells(star_index, total_count):
    bit_total = max(1, (total_count - 1).bit_length())
    lattice = [jnp.zeros_like(star_index), jnp.zeros_like(star_index), jnp.zeros_like(star_index)]
    extents = [1, 1, 1]
    for bit_pos in range(bit_total):
        axis_pick = bit_pos % 3
        depth_level = bit_pos // 3
        lattice[axis_pick] = lattice[axis_pick] + star_index // 2 ** bit_pos % 2 * 2 ** depth_level
        extents[axis_pick] = 2 ** (depth_level + 1)
    return (lattice, extents)


def draw_star_state(key, part):
    subkeys = jax.random.split(jax.random.fold_in(key, 202), 6)
    coarse_cell, field_at = coarse_layout(key)
    star_index = jnp.arange(STARS, dtype=jnp.int32)
    shard_index = star_index // FIELD_DEV
    cell_index = coarse_cell.reshape(-1)
    outer, outer_ext = lattice_cells(cell_index, FIELD_DEV)
    inner, inner_ext = lattice_cells(shard_index, N_BLK)
    spans = [outer_ext[0] * inner_ext[0], outer_ext[1] * inner_ext[1], outer_ext[2] * inner_ext[2]]
    spacing = 2.0 / max(spans)
    jitter = jnp.clip(0.15 * jax.random.normal(subkeys[1], (3, STARS), jnp.float32), -0.4, 0.4)
    velocity = 0.5 * jax.random.normal(subkeys[2], (3, STARS), jnp.float32)
    masses = jnp.exp(jax.random.uniform(subkeys[5], (1, STARS), jnp.float32, math.log(0.25), math.log(4.0))) / STARS
    rows = []
    for axis_pick in range(3):
        cell = outer[axis_pick] * inner_ext[axis_pick] + inner[axis_pick]
        rows.append((cell.astype(jnp.float32) + 0.5 - 0.5 * spans[axis_pick] + jitter[axis_pick]) * spacing)
    position = jnp.stack(rows, axis=0)
    accel_rows = jax.random.normal(subkeys[3], (3, STARS), jnp.float32)
    jerk_rows = jax.random.normal(subkeys[4], (3, STARS), jnp.float32)
    return jnp.concatenate([position, velocity, accel_rows, jerk_rows, masses], axis=0)


def setup_inputs(seed: int = 0) -> dict:
    key_list = jax.random.split(jax.random.key(seed), 5)
    return {
        "star_state": draw_star_state(jax.random.fold_in(key_list[4], 71), 0),
        "active_local": draw_active_local(jax.random.fold_in(key_list[4], 71), 0),
        "neighbours": draw_neighbours(jax.random.fold_in(key_list[4], 71), 0),
        "counts": draw_counts(jax.random.fold_in(key_list[4], 71), 0),
    }


time_step = 0.0078125
soften_sq = 0.001

def pair_terms(pos_self, vel_self, pos_other, vel_other, mass_other):
    offset_pos = pos_other - pos_self
    rel_vel = vel_other - vel_self
    dist_sq = offset_pos[0] * offset_pos[0] + offset_pos[1] * offset_pos[1] + offset_pos[2] * offset_pos[2] + soften_sq
    inverse = 1.0 / jnp.sqrt(dist_sq)
    strength = mass_other * inverse * inverse * inverse
    radial = (offset_pos[0] * rel_vel[0] + offset_pos[1] * rel_vel[1] + offset_pos[2] * rel_vel[2]) / dist_sq
    accel = strength * offset_pos
    jerk_term = strength * (rel_vel - 3.0 * radial * offset_pos)
    return jnp.concatenate([accel, jerk_term], axis=0)

def predict(star_rows):
    position = star_rows[0:3] + time_step * (star_rows[3:6] + time_step * (0.5 * star_rows[6:9] + time_step * star_rows[9:12] / 6.0))
    velocity = star_rows[3:6] + time_step * (star_rows[6:9] + 0.5 * time_step * star_rows[9:12])
    return jnp.concatenate([position, velocity, star_rows[12:13]], axis=0)

def correct(own_state, total_sum):
    half_step = 0.5 * time_step
    twelfth = time_step * time_step / 12.0
    new_vel = own_state[3:6] + half_step * (own_state[6:9] + total_sum[0:3]) + twelfth * (own_state[9:12] - total_sum[3:6])
    new_pos = own_state[0:3] + half_step * (own_state[3:6] + new_vel) + twelfth * (own_state[6:9] - total_sum[0:3])
    return jnp.concatenate([new_pos, new_vel], axis=0)

def reference(star_state, active_local, neighbours, counts):
    predicted = predict(star_state)
    device_idx = jnp.arange(ACTIVES, dtype=jnp.int32) // A_DEV
    global_id = (device_idx // N_GRP * FIELD_DEV + active_local).astype(jnp.int32)
    own_state = jnp.take(star_state, global_id, axis=1)
    actives = jnp.take(predicted, global_id, axis=1)[0:6]
    act_blocks = actives.reshape(6, ACTIVES // A_DEV, A_DEV).transpose(1, 0, 2)

    def regular_block(act_block):
        pair_vals = pair_terms(act_block[0:3, :, None], act_block[3:6, :, None], predicted[0:3, None, :], predicted[3:6, None, :], predicted[6][None, :])
        return lax.optimization_barrier(jnp.sum(pair_vals, axis=-1))
    total_sum = lax.map(regular_block, act_blocks).transpose(1, 0, 2).reshape(6, ACTIVES)
    entries = jnp.take(predicted, neighbours, axis=1)
    pair_vals = pair_terms(actives[0:3, :, None], actives[3:6, :, None], entries[0:3], entries[3:6], entries[6])
    live_mask = jnp.arange(NB, dtype=jnp.int32)[None, :] < counts[:, None]
    irregular = lax.optimization_barrier(jnp.sum(jnp.where(live_mask[None], pair_vals, 0.0), axis=-1))
    return (correct(own_state, total_sum), total_sum - irregular, irregular)
```

```python
import functools
import jax
import jax.numpy as jnp
from jax import lax
from jax.experimental import pallas as pl
from jax.experimental.pallas import tpu as pltpu
from jax.sharding import PartitionSpec as P

time_step = 0.0078125
soften_sq = 0.001
F32 = jnp.float32
I32 = jnp.int32
ZX = (0, 1, 3, 2)


def iota(shape, dim):
    return lax.broadcasted_iota(I32, shape, dim)


def lane_gather(table, lane):
    return jnp.take_along_axis(table, lane, axis=1, mode="promise_in_bounds")


def pair_terms(other, own, acc):
    dx = [other[c] - own[c] for c in range(3)]
    dv = [other[3 + c] - own[3 + c] for c in range(3)]
    dist = dx[0] * dx[0] + dx[1] * dx[1] + (dx[2] * dx[2] + soften_sq)
    inv = lax.rsqrt(dist)
    radial = dx[0] * dv[0] + dx[1] * dv[1] + dx[2] * dv[2]
    inv2 = inv * inv
    w = (other[6] * inv) * inv2
    q = radial * inv2
    for c in range(3):
        wx = w * dx[c]
        acc[c] = acc[c] + wx
        acc[3 + c] = acc[3 + c] + w * dv[c]
        acc[6 + c] = acc[6 + c] + q * wx
    return acc


def finish(acc):
    return list(acc[:3]) + [acc[3 + c] - 3.0 * acc[6 + c] for c in range(3)]


def prep_kernel(state, local, nb, counts, stars, pack, own):
    h = time_step
    x, v, a, j = (state[3 * k : 3 * k + 3, :] for k in range(4))
    pos = x + h * (v + h * (0.5 * a + h * j / 6.0))
    vel = v + h * (a + 0.5 * h * j)
    pred = jnp.concatenate([pos, vel, state[12:13, :], jnp.zeros((1, 512), F32)], axis=0)
    stars[...] = pred
    idx = local[...]
    idx = jnp.broadcast_to(jnp.concatenate([idx, idx], axis=1), (8, 128))
    part = idx >> 7
    lane = idx & 127
    low = state[0:8, :]
    high = jnp.concatenate([state[8:13, :], jnp.zeros((3, 512), F32)], axis=0)

    def pick(rows):
        out = lane_gather(rows[:, 0:128], lane)
        for k in range(1, 4):
            out = jnp.where(part == k, lane_gather(rows[:, 128 * k : 128 * k + 128], lane), out)
        return out

    pack[32:40, :] = pick(pred)
    own[0:8, :] = pick(low)
    own[8:16, :] = pick(high)
    ids = nb[...].astype(F32)
    ids = jnp.concatenate([ids, ids], axis=1)
    ids = jnp.transpose(ids)
    half = iota((32, 128), 1) // 64
    cnt = counts[...]
    cnt = jnp.concatenate([cnt, cnt], axis=1)
    both = jnp.concatenate([ids[0:32, :], ids[32:64, :]], axis=1)
    live = iota((32, 128), 0) + 32 * half < cnt
    pack[0:32, :] = jnp.where(live, both, -1.0)


def pair_loop(stars, rows, ab, racc, count):
    sets = len(rows)
    for t in range(sets):
        cols = jnp.transpose(rows[t])
        for c in range(6):
            ab[c, t * 128 : t * 128 + 128, :] = jnp.broadcast_to(cols[:, c : c + 1], (128, 128))

    def octets(g, carry):
        at = [pl.ds(pl.multiple_of(g * 16 + 8 * t, 8), 8) for t in range(2)]
        own = [[ab[c, at[t], :] for c in range(6)] for t in range(2)]

        def shard(b, acc):
            acc = list(acc)
            for k in range(4):
                lanes = slice(128 * k, 128 * k + 128)
                other = [jnp.broadcast_to(stars[b, c : c + 1, lanes], (8, 128)) for c in range(7)]
                for t in range(2):
                    acc[9 * t : 9 * t + 9] = pair_terms(other, own[t], acc[9 * t : 9 * t + 9])
            return tuple(acc)

        acc = lax.fori_loop(0, count, shard, (jnp.zeros((8, 128), F32),) * 18)
        for t in range(2):
            for k, val in enumerate(finish(acc[9 * t : 9 * t + 9])):
                racc[k, at[t], :] = val
        return carry

    lax.fori_loop(0, sets * 8, octets, 0)
    lane = iota((128, 128), 1)
    sums = []
    for t in range(sets):
        cols = jnp.zeros((128, 128), F32)
        for k in range(6):
            part = racc[k, t * 128 : t * 128 + 128, :]
            cols = jnp.where(lane == k, jnp.sum(part, axis=1, keepdims=True), cols)
        sums.append(jnp.transpose(cols)[0:8, :])
    return sums


def rows_of(pack):
    lane = iota((8, 128), 1)
    return jnp.where(lane < 64, pack[0, 32:40, :], pack[1, 32:40, :])


def near_kernel(stars, near, far, out, ab, racc):
    sums = pair_loop(stars, [rows_of(near), rows_of(far)], ab, racc, 8)
    out[0] = sums[0]
    out[1] = sums[1]


def irregular(blk, pack, tables):
    row = iota((8, 128), 0)
    zx = (row & 3) ^ ((row & 3) >> 1)
    shard0 = blk ^ ((zx << 1) ^ (row >> 2))
    owners = [shard0.astype(F32), (shard0 ^ 32).astype(F32)]
    out = []
    for t in range(2):
        ids = pack[t, 0:32, :]
        owner = jnp.floor(ids * (1.0 / 512.0))
        local = ids - 512.0 * owner
        act = pack[t, 32:40, :]
        own = [jnp.broadcast_to(act[c : c + 1, :], (8, 128)) for c in range(6)]
        zero = jnp.zeros((8, 128), F32)
        owner_rows = [jnp.broadcast_to(owner[k : k + 1, :], (8, 128)) for k in range(32)]
        local_rows = [jnp.broadcast_to(local[k : k + 1, :], (8, 128)) for k in range(32)]

        def scan(layer):
            found = []
            for u in range(2):
                seen, pos = zero, zero
                for k in range(32):
                    hit = owner_rows[k] == owners[u]
                    pos = jnp.where(hit & (seen == layer), local_rows[k], pos)
                    seen = jnp.where(hit, seen + 1.0, seen)
                found.append((seen, pos))
            return found

        def add(layer, acc):
            level = layer.astype(F32)
            acc = list(acc)
            for u, (seen, pos) in enumerate(scan(level)):
                idx = pos.astype(I32)
                part = idx >> 7
                lane = idx & 127
                other = []
                for c in range(7):
                    got = lane_gather(tables[u][:, c, 0:128], lane)
                    for k in range(1, 4):
                        tab = tables[u][:, c, 128 * k : 128 * k + 128]
                        got = jnp.where(part == k, lane_gather(tab, lane), got)
                    other.append(got)
                other[6] = jnp.where(seen > level, other[6], 0.0)
                acc = pair_terms(other, own, acc)
            return tuple(acc)

        most = zero
        for u in range(2):
            seen = zero
            for k in range(32):
                seen = jnp.where(owner_rows[k] == owners[u], seen + 1.0, seen)
            most = jnp.maximum(most, seen)
        layers = jnp.max(most).astype(I32)
        acc = lax.fori_loop(0, layers, add, (zero,) * 9)
        sums = jnp.concatenate([jnp.sum(r, axis=0, keepdims=True) for r in finish(acc)], axis=0)
        out.append(sums + pltpu.roll(sums, 64, 1))
    lane = iota((6, 128), 1)
    return jnp.where(lane < 64, out[0], out[1])


def last_kernel(blk, first, second, pack, before, out, ab, racc):
    (sums,) = pair_loop(second, [rows_of(pack)], ab, racc, 8)
    irr = irregular(blk[0], pack, (first, second))
    out[0:6, :] = (sums + before[...])[0:6, :]
    out[6:12, :] = irr
    out[12:16, :] = jnp.zeros((4, 128), F32)


def final_kernel(own, near, got, new, regular, irr):
    lane64 = slice(0, 64)
    every = near[:, lane64] + got[:, 64:128]
    total = every[0:6]
    state = own[:, lane64]
    half = 0.5 * time_step
    twelfth = time_step * time_step / 12.0
    vel = state[3:6] + half * (state[6:9] + total[0:3]) + twelfth * (state[9:12] - total[3:6])
    pos = state[0:3] + half * (state[3:6] + vel) + twelfth * (state[6:9] - total[0:3])
    new[...] = jnp.concatenate([pos, vel], axis=0)
    irr[...] = every[6:12]
    regular[...] = total - every[6:12]


def shape(*dims):
    return jax.ShapeDtypeStruct(dims, F32)


def exchange(value, mask):
    return lax.ppermute(value, "blk", [(b, b ^ mask) for b in range(64)])


def per_device(star_state, active_local, neighbours, counts):
    blk = lax.axis_index("blk").astype(I32).reshape(1)
    stars, pack, own = pl.pallas_call(
        prep_kernel, out_shape=(shape(8, 512), shape(40, 128), shape(16, 128)), name="prep"
    )(star_state, active_local.reshape(1, 64), neighbours, counts.reshape(1, 64))
    stars2 = jnp.stack([stars, exchange(stars, 2)])
    near = jnp.stack([pack, exchange(pack, 8)])
    stars4 = jnp.concatenate([stars2, exchange(stars2, 6)])
    far = exchange(near, 24)
    stars8 = jnp.concatenate([stars4, exchange(stars4, 1)])
    other8 = exchange(stars8, 32)
    scratch = lambda n: [pltpu.VMEM((6, n, 128), F32), pltpu.VMEM((6, n, 128), F32)]
    before = pl.pallas_call(
        near_kernel, out_shape=shape(2, 8, 128), scratch_shapes=scratch(256), name="pairs_a"
    )(stars8, near, far)
    smem = pl.BlockSpec(memory_space=pltpu.SMEM)
    vmem = pl.BlockSpec(memory_space=pltpu.VMEM)

    def last(pack, part, name):
        return pl.pallas_call(
            last_kernel,
            in_specs=[smem, vmem, vmem, vmem, vmem],
            out_shape=shape(16, 128),
            scratch_shapes=scratch(128),
            name=name,
        )(blk, stars8, other8, pack, part)

    far_sum = last(far, before[1], "pairs_far")
    got_far = exchange(far_sum, 24)
    near_sum = last(near, before[0], "pairs_near") + got_far
    got_near = exchange(near_sum, 8)
    return pl.pallas_call(
        final_kernel, out_shape=(shape(6, 64), shape(6, 64), shape(6, 64)), name="final"
    )(own, near_sum, got_near)


def solution(mesh):
    in_specs = (P(None, "blk"), P(("blk", "grp")), P(("blk", "grp"), None), P(("blk", "grp")))
    out_specs = (P(None, ("blk", "grp")), P(None, ("blk", "grp")), P(None, ("blk", "grp")))
    return jax.shard_map(
        per_device, mesh=mesh, in_specs=in_specs, out_specs=out_specs, check_vma=False
    )
```

```python
import functools
import jax
import jax.numpy as jnp
from jax import lax
from jax.experimental import pallas as pl
from jax.experimental.pallas import tpu as pltpu
from jax.sharding import PartitionSpec as P

time_step = 0.0078125
soften_sq = 0.001
F32 = jnp.float32
I32 = jnp.int32
ZX = (0, 1, 3, 2)


def iota(shape, dim):
    return lax.broadcasted_iota(I32, shape, dim)


def lane_gather(table, lane):
    return jnp.take_along_axis(table, lane, axis=1, mode="promise_in_bounds")


def pair_terms(other, own, acc):
    dx = [other[c] - own[c] for c in range(3)]
    dv = [other[3 + c] - own[3 + c] for c in range(3)]
    dist = dx[0] * dx[0] + dx[1] * dx[1] + (dx[2] * dx[2] + soften_sq)
    inv = lax.rsqrt(dist)
    radial = dx[0] * dv[0] + dx[1] * dv[1] + dx[2] * dv[2]
    inv2 = inv * inv
    w = (other[6] * inv) * inv2
    q = radial * inv2
    for c in range(3):
        wx = w * dx[c]
        acc[c] = acc[c] + wx
        acc[3 + c] = acc[3 + c] + w * dv[c]
        acc[6 + c] = acc[6 + c] + q * wx
    return acc


def finish(acc):
    return list(acc[:3]) + [acc[3 + c] - 3.0 * acc[6 + c] for c in range(3)]


def prep_kernel(state, local, nb, counts, stars, pack, own):
    h = time_step
    x, v, a, j = (state[3 * k : 3 * k + 3, :] for k in range(4))
    pos = x + h * (v + h * (0.5 * a + h * j / 6.0))
    vel = v + h * (a + 0.5 * h * j)
    pred = jnp.concatenate([pos, vel, state[12:13, :], jnp.zeros((1, 512), F32)], axis=0)
    stars[...] = pred
    idx = local[...]
    idx = jnp.broadcast_to(jnp.concatenate([idx, idx], axis=1), (8, 128))
    part = idx >> 7
    lane = idx & 127
    low = state[0:8, :]
    high = jnp.concatenate([state[8:13, :], jnp.zeros((3, 512), F32)], axis=0)

    def pick(rows):
        out = lane_gather(rows[:, 0:128], lane)
        for k in range(1, 4):
            out = jnp.where(part == k, lane_gather(rows[:, 128 * k : 128 * k + 128], lane), out)
        return out

    pack[32:40, :] = pick(pred)
    own[0:8, :] = pick(low)
    own[8:16, :] = pick(high)
    ids = nb[...].astype(F32)
    ids = jnp.concatenate([ids, ids], axis=1)
    ids = jnp.transpose(ids)
    half = iota((32, 128), 1) // 64
    cnt = counts[...]
    cnt = jnp.concatenate([cnt, cnt], axis=1)
    both = jnp.concatenate([ids[0:32, :], ids[32:64, :]], axis=1)
    live = iota((32, 128), 0) + 32 * half < cnt
    pack[0:32, :] = jnp.where(live, both, -1.0)


def pair_loop(stars, rows, ab, racc, count):
    sets = len(rows)
    for t in range(sets):
        cols = jnp.transpose(rows[t])
        for c in range(6):
            ab[c, t * 128 : t * 128 + 128, :] = jnp.broadcast_to(cols[:, c : c + 1], (128, 128))

    def octets(g, carry):
        at = [pl.ds(pl.multiple_of(g * 16 + 8 * t, 8), 8) for t in range(2)]
        own = [[ab[c, at[t], :] for c in range(6)] for t in range(2)]

        def shard(b, acc):
            acc = list(acc)
            for k in range(4):
                lanes = slice(128 * k, 128 * k + 128)
                other = [jnp.broadcast_to(stars[b, c : c + 1, lanes], (8, 128)) for c in range(7)]
                for t in range(2):
                    acc[9 * t : 9 * t + 9] = pair_terms(other, own[t], acc[9 * t : 9 * t + 9])
            return tuple(acc)

        acc = lax.fori_loop(0, count, shard, (jnp.zeros((8, 128), F32),) * 18)
        for t in range(2):
            for k, val in enumerate(finish(acc[9 * t : 9 * t + 9])):
                racc[k, at[t], :] = val
        return carry

    lax.fori_loop(0, sets * 8, octets, 0)
    lane = iota((128, 128), 1)
    sums = []
    for t in range(sets):
        cols = jnp.zeros((128, 128), F32)
        for k in range(6):
            part = racc[k, t * 128 : t * 128 + 128, :]
            cols = jnp.where(lane == k, jnp.sum(part, axis=1, keepdims=True), cols)
        sums.append(jnp.transpose(cols)[0:8, :])
    return sums


def rows_of(pack):
    lane = iota((8, 128), 1)
    return jnp.where(lane < 64, pack[0, 32:40, :], pack[1, 32:40, :])


def first_kernel(stars, near, far, near_out, far_out, ab, racc):
    sums = pair_loop(stars, [rows_of(near), rows_of(far)], ab, racc, 8)
    near_out[...] = sums[0]
    far_out[...] = sums[1]


def irregular(blk, pack, tables):
    row = iota((8, 128), 0)
    zx = (row & 3) ^ ((row & 3) >> 1)
    shard0 = blk ^ ((zx << 1) ^ (row >> 2))
    owners = [shard0.astype(F32), (shard0 ^ 32).astype(F32)]
    out = []
    for t in range(2):
        ids = pack[t, 0:32, :]
        owner = jnp.floor(ids * (1.0 / 512.0))
        local = ids - 512.0 * owner
        act = pack[t, 32:40, :]
        own = [jnp.broadcast_to(act[c : c + 1, :], (8, 128)) for c in range(6)]
        zero = jnp.zeros((8, 128), F32)
        owner_rows = [jnp.broadcast_to(owner[k : k + 1, :], (8, 128)) for k in range(32)]
        local_rows = [jnp.broadcast_to(local[k : k + 1, :], (8, 128)) for k in range(32)]

        def scan(layer):
            found = []
            for u in range(2):
                seen, pos = zero, zero
                for k in range(32):
                    hit = owner_rows[k] == owners[u]
                    pos = jnp.where(hit & (seen == layer), local_rows[k], pos)
                    seen = jnp.where(hit, seen + 1.0, seen)
                found.append((seen, pos))
            return found

        def add(layer, acc):
            level = layer.astype(F32)
            acc = list(acc)
            for u, (seen, pos) in enumerate(scan(level)):
                idx = pos.astype(I32)
                part = idx >> 7
                lane = idx & 127
                other = []
                for c in range(7):
                    got = lane_gather(tables[u][:, c, 0:128], lane)
                    for k in range(1, 4):
                        tab = tables[u][:, c, 128 * k : 128 * k + 128]
                        got = jnp.where(part == k, lane_gather(tab, lane), got)
                    other.append(got)
                other[6] = jnp.where(seen > level, other[6], 0.0)
                acc = pair_terms(other, own, acc)
            return tuple(acc)

        most = zero
        for u in range(2):
            seen = zero
            for k in range(32):
                seen = jnp.where(owner_rows[k] == owners[u], seen + 1.0, seen)
            most = jnp.maximum(most, seen)
        layers = jnp.max(most).astype(I32)
        acc = lax.fori_loop(0, layers, add, (zero,) * 9)
        sums = jnp.concatenate([jnp.sum(r, axis=0, keepdims=True) for r in finish(acc)], axis=0)
        out.append(sums + pltpu.roll(sums, 64, 1))
    lane = iota((6, 128), 1)
    return jnp.where(lane < 64, out[0], out[1])


def last_kernel(blk, first, second, pack, before, out, ab, racc):
    (sums,) = pair_loop(second, [rows_of(pack)], ab, racc, 8)
    irr = irregular(blk[0], pack, (first, second))
    out[0:6, :] = (sums + before[...])[0:6, :]
    out[6:12, :] = irr
    out[12:16, :] = jnp.zeros((4, 128), F32)


def final_kernel(own, near, got, new, regular, irr):
    lane64 = slice(0, 64)
    every = near[:, lane64] + got[:, 64:128]
    total = every[0:6]
    state = own[:, lane64]
    half = 0.5 * time_step
    twelfth = time_step * time_step / 12.0
    vel = state[3:6] + half * (state[6:9] + total[0:3]) + twelfth * (state[9:12] - total[3:6])
    pos = state[0:3] + half * (state[3:6] + vel) + twelfth * (state[6:9] - total[0:3])
    new[...] = jnp.concatenate([pos, vel], axis=0)
    irr[...] = every[6:12]
    regular[...] = total - every[6:12]


def shape(*dims):
    return jax.ShapeDtypeStruct(dims, F32)


def near_memory(*dims):
    return pltpu.VMEM(dims, F32)


def held(*values):
    return [pltpu.with_memory_space_constraint(v, pltpu.VMEM) for v in values]


def exchange(value, mask):
    return lax.ppermute(value, "blk", [(b, b ^ mask) for b in range(64)])


def per_device(star_state, active_local, neighbours, counts):
    blk = lax.axis_index("blk").astype(I32).reshape(1)
    stars, pack, own = pl.pallas_call(
        prep_kernel,
        out_shape=(near_memory(8, 512), near_memory(40, 128), near_memory(16, 128)),
        name="prep",
    )(star_state, active_local.reshape(1, 64), neighbours, counts.reshape(1, 64))
    got = lax.optimization_barrier((exchange(stars, 2), exchange(pack, 8)))
    stars2 = jnp.stack([stars, got[0]])
    near = jnp.stack([pack, got[1]])
    got = lax.optimization_barrier((exchange(stars2, 6), exchange(near, 24)))
    stars4 = jnp.concatenate([stars2, got[0]])
    far = got[1]
    stars8 = jnp.concatenate([stars4, exchange(stars4, 1)])
    other8 = exchange(stars8, 32)
    scratch = lambda n: [pltpu.VMEM((6, n, 128), F32), pltpu.VMEM((6, n, 128), F32)]
    near_part, far_part = pl.pallas_call(
        first_kernel,
        out_shape=(near_memory(8, 128), near_memory(8, 128)),
        scratch_shapes=scratch(256),
        name="pairs_a",
    )(*held(stars8, near, far))
    smem = pl.BlockSpec(memory_space=pltpu.SMEM)
    vmem = pl.BlockSpec(memory_space=pltpu.VMEM)

    def last(pack, part, name):
        return pl.pallas_call(
            last_kernel,
            in_specs=[smem, vmem, vmem, vmem, vmem],
            out_shape=near_memory(16, 128),
            scratch_shapes=scratch(128),
            name=name,
        )(blk, *held(stars8, other8, pack, part))

    far_sum = last(far, far_part, "pairs_far")
    got_far = exchange(far_sum, 24)
    near_sum = last(near, near_part, "pairs_near") + got_far
    got_near = exchange(near_sum, 8)
    return pl.pallas_call(
        final_kernel, out_shape=(shape(6, 64), shape(6, 64), shape(6, 64)), name="final"
    )(*held(own, near_sum, got_near))


def solution(mesh):
    in_specs = (P(None, "blk"), P(("blk", "grp")), P(("blk", "grp"), None), P(("blk", "grp")))
    out_specs = (P(None, ("blk", "grp")), P(None, ("blk", "grp")), P(None, ("blk", "grp")))
    return jax.shard_map(
        per_device, mesh=mesh, in_specs=in_specs, out_specs=out_specs, check_vma=False
    )
```

```python
import functools
import jax
import jax.numpy as jnp
from jax import lax
from jax.experimental import pallas as pl
from jax.experimental.pallas import tpu as pltpu
from jax.sharding import PartitionSpec as P

time_step = 0.0078125
soften_sq = 0.001
F32 = jnp.float32
I32 = jnp.int32


def iota(shape, dim):
    return lax.broadcasted_iota(I32, shape, dim)


def lane_gather(table, lane):
    return jnp.take_along_axis(table, lane, axis=1, mode="promise_in_bounds")


def pair_terms(other, own, acc):
    dx = [other[c] - own[c] for c in range(3)]
    dv = [other[3 + c] - own[3 + c] for c in range(3)]
    dist = dx[0] * dx[0] + dx[1] * dx[1] + (dx[2] * dx[2] + soften_sq)
    inv = lax.rsqrt(dist)
    radial = dx[0] * dv[0] + dx[1] * dv[1] + dx[2] * dv[2]
    inv2 = inv * inv
    w = (other[6] * inv) * inv2
    q = radial * inv2
    for c in range(3):
        wx = w * dx[c]
        acc[c] = acc[c] + wx
        acc[3 + c] = acc[3 + c] + w * dv[c]
        acc[6 + c] = acc[6 + c] + q * wx
    return acc


def finish(acc):
    return list(acc[:3]) + [acc[3 + c] - 3.0 * acc[6 + c] for c in range(3)]


def prep_kernel(state, local, nb, counts, stars, pack, own):
    h = time_step
    x, v, a, j = (state[3 * k : 3 * k + 3, :] for k in range(4))
    pos = x + h * (v + h * (0.5 * a + h * j / 6.0))
    vel = v + h * (a + 0.5 * h * j)
    pred = jnp.concatenate([pos, vel, state[12:13, :], jnp.zeros((1, 512), F32)], axis=0)
    stars[...] = pred
    idx = local[...]
    idx = jnp.broadcast_to(jnp.concatenate([idx, idx], axis=1), (8, 128))
    part = idx >> 7
    lane = idx & 127
    low = state[0:8, :]
    high = jnp.concatenate([state[8:13, :], jnp.zeros((3, 512), F32)], axis=0)

    def pick(rows):
        out = lane_gather(rows[:, 0:128], lane)
        for k in range(1, 4):
            out = jnp.where(part == k, lane_gather(rows[:, 128 * k : 128 * k + 128], lane), out)
        return out

    pack[32:40, :] = pick(pred)
    own[0:8, :] = pick(low)
    own[8:16, :] = pick(high)
    ids = nb[...].astype(F32)
    ids = jnp.concatenate([ids, ids], axis=1)
    ids = jnp.transpose(ids)
    half = iota((32, 128), 1) // 64
    cnt = counts[...]
    cnt = jnp.concatenate([cnt, cnt], axis=1)
    both = jnp.concatenate([ids[0:32, :], ids[32:64, :]], axis=1)
    live = iota((32, 128), 0) + 32 * half < cnt
    pack[0:32, :] = jnp.where(live, both, -1.0)


def spread(rows, ab):
    cols = jnp.transpose(rows)
    for c in range(6):
        ab[c] = jnp.broadcast_to(cols[:, c : c + 1], (128, 128))


def pair_loop(stars, ab, before, out):
    count = stars.shape[0]

    def octets(g, carry):
        at = [pl.ds(pl.multiple_of(g * 16 + 8 * t, 8), 8) for t in range(2)]
        own = [[ab[c, at[t], :] for c in range(6)] for t in range(2)]

        def shard(b, acc):
            acc = list(acc)
            for k in range(4):
                lanes = slice(128 * k, 128 * k + 128)
                other = [jnp.broadcast_to(stars[b, c : c + 1, lanes], (8, 128)) for c in range(7)]
                for t in range(2):
                    acc[9 * t : 9 * t + 9] = pair_terms(other, own[t], acc[9 * t : 9 * t + 9])
            return tuple(acc)

        acc = lax.fori_loop(0, count, shard, (jnp.zeros((8, 128), F32),) * 18)
        for t in range(2):
            for k, val in enumerate(finish(acc[9 * t : 9 * t + 9])):
                out[k, at[t], :] = val if before is None else val + before[k, at[t], :]
        return carry

    lax.fori_loop(0, 8, octets, 0)


def lane_sums(racc):
    lane = iota((128, 128), 1)
    cols = jnp.zeros((128, 128), F32)
    for k in range(6):
        cols = jnp.where(lane == k, jnp.sum(racc[k], axis=1, keepdims=True), cols)
    return jnp.transpose(cols)[0:8, :]


def rows_of(pack):
    lane = iota((8, 128), 1)
    return jnp.where(lane < 64, pack[0, 32:40, :], pack[1, 32:40, :])


def pairs_two(stars, near, ab, out, token):
    token[...] = jnp.zeros((8, 128), F32)
    spread(rows_of(near), ab)
    pair_loop(stars, ab, None, out)


def pairs_four(got, stars, far, ab_near, near_in, after, ab_far, sums, racc):
    pair_loop(got, ab_near, near_in, racc)
    sums[0] = lane_sums(racc) + after[...]
    spread(rows_of(far), ab_far)
    pair_loop(stars, ab_far, None, racc)
    sums[1] = lane_sums(racc)


def pairs_eight(got, ab_near, ab_far, near_out, far_out):
    pair_loop(got, ab_far, None, far_out)
    pair_loop(got, ab_near, None, near_out)


def irregular(blk, pack, tables):
    row = iota((8, 128), 0)
    z = (row >> 1) ^ (row >> 2)
    shard0 = blk ^ ((z << 1) ^ (row & 1))
    owners = [shard0.astype(F32), (shard0 ^ 32).astype(F32)]
    out = []
    for t in range(2):
        ids = pack[t, 0:32, :]
        owner = jnp.floor(ids * (1.0 / 512.0))
        local = ids - 512.0 * owner
        act = pack[t, 32:40, :]
        own = [jnp.broadcast_to(act[c : c + 1, :], (8, 128)) for c in range(6)]
        zero = jnp.zeros((8, 128), F32)
        owner_rows = [jnp.broadcast_to(owner[k : k + 1, :], (8, 128)) for k in range(32)]
        local_rows = [jnp.broadcast_to(local[k : k + 1, :], (8, 128)) for k in range(32)]

        def scan(layer):
            found = []
            for u in range(2):
                seen, pos = zero, zero
                for k in range(32):
                    hit = owner_rows[k] == owners[u]
                    pos = jnp.where(hit & (seen == layer), local_rows[k], pos)
                    seen = jnp.where(hit, seen + 1.0, seen)
                found.append((seen, pos))
            return found

        def add(layer, acc):
            level = layer.astype(F32)
            acc = list(acc)
            for u, (seen, pos) in enumerate(scan(level)):
                idx = pos.astype(I32)
                part = idx >> 7
                lane = idx & 127
                other = []
                for c in range(7):
                    got = lane_gather(tables[u][:, c, 0:128], lane)
                    for k in range(1, 4):
                        tab = tables[u][:, c, 128 * k : 128 * k + 128]
                        got = jnp.where(part == k, lane_gather(tab, lane), got)
                    other.append(got)
                other[6] = jnp.where(seen > level, other[6], 0.0)
                acc = pair_terms(other, own, acc)
            return tuple(acc)

        most = zero
        for u in range(2):
            seen = zero
            for k in range(32):
                seen = jnp.where(owner_rows[k] == owners[u], seen + 1.0, seen)
            most = jnp.maximum(most, seen)
        layers = jnp.max(most).astype(I32)
        acc = lax.fori_loop(0, layers, add, (zero,) * 9)
        sums = jnp.concatenate([jnp.sum(r, axis=0, keepdims=True) for r in finish(acc)], axis=0)
        out.append(sums + pltpu.roll(sums, 64, 1))
    lane = iota((6, 128), 1)
    return jnp.where(lane < 64, out[0], out[1])


def last_kernel(which, blk, first, second, pack, ab, before, sums, out, racc):
    pair_loop(second, ab, before, racc)
    irr = irregular(blk[0], pack, (first, second))
    out[0:6, :] = (lane_sums(racc) + sums[which])[0:6, :]
    out[6:12, :] = irr
    out[12:16, :] = jnp.zeros((4, 128), F32)


def final_kernel(own, near, got, new, regular, irr):
    lane64 = slice(0, 64)
    every = near[:, lane64] + got[:, 64:128]
    total = every[0:6]
    state = own[:, lane64]
    half = 0.5 * time_step
    twelfth = time_step * time_step / 12.0
    vel = state[3:6] + half * (state[6:9] + total[0:3]) + twelfth * (state[9:12] - total[3:6])
    pos = state[0:3] + half * (state[3:6] + vel) + twelfth * (state[6:9] - total[0:3])
    new[...] = jnp.concatenate([pos, vel], axis=0)
    irr[...] = every[6:12]
    regular[...] = total - every[6:12]


def shape(*dims):
    return jax.ShapeDtypeStruct(dims, F32)


def near_memory(*dims):
    return pltpu.VMEM(dims, F32)


def held(*values):
    return [pltpu.with_memory_space_constraint(v, pltpu.VMEM) for v in values]


def exchange(value, mask):
    return lax.ppermute(value, "blk", [(b, b ^ mask) for b in range(64)])


def per_device(star_state, active_local, neighbours, counts):
    blk = lax.axis_index("blk").astype(I32).reshape(1)
    stars, pack, own = pl.pallas_call(
        prep_kernel,
        out_shape=(near_memory(8, 512), near_memory(40, 128), near_memory(16, 128)),
        name="prep",
    )(star_state, active_local.reshape(1, 64), neighbours, counts.reshape(1, 64))
    got = lax.optimization_barrier((exchange(stars, 1), exchange(pack, 8)))
    stars2 = jnp.stack([stars, got[0]])
    near = jnp.stack([pack, got[1]])
    block = near_memory(6, 128, 128)
    small = near_memory(8, 128)
    ab_near, near2, token = pl.pallas_call(
        pairs_two, out_shape=(block, block, small), name="pairs_two"
    )(*held(stars2, near))
    far, got2, token = lax.optimization_barrier((exchange(near, 24), exchange(stars2, 2), token))
    stars4 = jnp.concatenate([stars2, got2])
    ab_far, sums4 = pl.pallas_call(
        pairs_four,
        out_shape=(block, near_memory(2, 8, 128)),
        scratch_shapes=[pltpu.VMEM((6, 128, 128), F32)],
        name="pairs_four",
    )(*held(got2, stars4, far, ab_near, near2, token))
    got4, sums4 = lax.optimization_barrier((exchange(stars4, 6), sums4))
    stars8 = jnp.concatenate([stars4, got4])
    other8 = exchange(stars8, 32)
    near8, far8 = pl.pallas_call(pairs_eight, out_shape=(block, block), name="pairs_eight")(
        *held(got4, ab_near, ab_far)
    )
    smem = pl.BlockSpec(memory_space=pltpu.SMEM)
    vmem = pl.BlockSpec(memory_space=pltpu.VMEM)

    def last(which, pack, ab, part, name):
        return pl.pallas_call(
            functools.partial(last_kernel, which),
            in_specs=[smem] + [vmem] * 6,
            out_shape=near_memory(16, 128),
            scratch_shapes=[pltpu.VMEM((6, 128, 128), F32)],
            name=name,
        )(blk, *held(stars8, other8, pack, ab, part, sums4))

    far_sum = last(1, far, ab_far, far8, "pairs_far")
    got_far = exchange(far_sum, 24)
    near_sum = last(0, near, ab_near, near8, "pairs_near") + got_far
    got_near = exchange(near_sum, 8)
    return pl.pallas_call(
        final_kernel, out_shape=(shape(6, 64), shape(6, 64), shape(6, 64)), name="final"
    )(*held(own, near_sum, got_near))


def solution(mesh):
    in_specs = (P(None, "blk"), P(("blk", "grp")), P(("blk", "grp"), None), P(("blk", "grp")))
    out_specs = (P(None, ("blk", "grp")), P(None, ("blk", "grp")), P(None, ("blk", "grp")))
    return jax.shard_map(
        per_device, mesh=mesh, in_specs=in_specs, out_specs=out_specs, check_vma=False
    )
```

```python
import functools
import jax
import jax.numpy as jnp
from jax import lax
from jax.experimental import pallas as pl
from jax.experimental.pallas import tpu as pltpu
from jax.sharding import PartitionSpec as P

time_step = 0.0078125
soften_sq = 0.001
F32 = jnp.float32
I32 = jnp.int32


def iota(shape, dim):
    return lax.broadcasted_iota(I32, shape, dim)


def lane_gather(table, lane):
    return jnp.take_along_axis(table, lane, axis=1, mode="promise_in_bounds")


def pair_terms(other, own, acc):
    dx = [other[c] - own[c] for c in range(3)]
    dv = [other[3 + c] - own[3 + c] for c in range(3)]
    dist = dx[0] * dx[0] + dx[1] * dx[1] + (dx[2] * dx[2] + soften_sq)
    inv = lax.rsqrt(dist)
    radial = dx[0] * dv[0] + dx[1] * dv[1] + dx[2] * dv[2]
    inv2 = inv * inv
    w = (other[6] * inv) * inv2
    q = radial * inv2
    for c in range(3):
        wx = w * dx[c]
        acc[c] = acc[c] + wx
        acc[3 + c] = acc[3 + c] + w * dv[c]
        acc[6 + c] = acc[6 + c] + q * wx
    return acc


def finish(acc):
    return list(acc[:3]) + [acc[3 + c] - 3.0 * acc[6 + c] for c in range(3)]


def prep_kernel(state, local, nb, counts, stars, pack, own):
    h = time_step
    x, v, a, j = (state[3 * k : 3 * k + 3, :] for k in range(4))
    pos = x + h * (v + h * (0.5 * a + h * j / 6.0))
    vel = v + h * (a + 0.5 * h * j)
    pred = jnp.concatenate([pos, vel, state[12:13, :], jnp.zeros((1, 512), F32)], axis=0)
    stars[...] = pred
    idx = local[...]
    idx = jnp.broadcast_to(jnp.concatenate([idx, idx], axis=1), (8, 128))
    part = idx >> 7
    lane = idx & 127
    low = state[0:8, :]
    high = jnp.concatenate([state[8:13, :], jnp.zeros((3, 512), F32)], axis=0)

    def pick(rows):
        out = lane_gather(rows[:, 0:128], lane)
        for k in range(1, 4):
            out = jnp.where(part == k, lane_gather(rows[:, 128 * k : 128 * k + 128], lane), out)
        return out

    pack[32:40, :] = pick(pred)
    own[0:8, :] = pick(low)
    own[8:16, :] = pick(high)
    ids = nb[...].astype(F32)
    ids = jnp.concatenate([ids, ids], axis=1)
    ids = jnp.transpose(ids)
    half = iota((32, 128), 1) // 64
    cnt = counts[...]
    cnt = jnp.concatenate([cnt, cnt], axis=1)
    both = jnp.concatenate([ids[0:32, :], ids[32:64, :]], axis=1)
    live = iota((32, 128), 0) + 32 * half < cnt
    pack[0:32, :] = jnp.where(live, both, -1.0)


def spread(rows, ab):
    cols = jnp.transpose(rows)
    for c in range(6):
        ab[c] = jnp.broadcast_to(cols[:, c : c + 1], (128, 128))


def pair_loop(stars, ab, before, out):
    count = stars.shape[0]

    def octets(g, carry):
        at = [pl.ds(pl.multiple_of(g * 16 + 8 * t, 8), 8) for t in range(2)]
        own = [[ab[c, at[t], :] for c in range(6)] for t in range(2)]

        def shard(b, acc):
            acc = list(acc)
            for k in range(4):
                lanes = slice(128 * k, 128 * k + 128)
                other = [jnp.broadcast_to(stars[b, c : c + 1, lanes], (8, 128)) for c in range(7)]
                for t in range(2):
                    acc[9 * t : 9 * t + 9] = pair_terms(other, own[t], acc[9 * t : 9 * t + 9])
            return tuple(acc)

        acc = lax.fori_loop(0, count, shard, (jnp.zeros((8, 128), F32),) * 18)
        for t in range(2):
            for k, val in enumerate(finish(acc[9 * t : 9 * t + 9])):
                out[k, at[t], :] = val if before is None else val + before[k, at[t], :]
        return carry

    lax.fori_loop(0, 8, octets, 0)


def lane_sums(racc):
    lane = iota((128, 128), 1)
    cols = jnp.zeros((128, 128), F32)
    for k in range(6):
        cols = jnp.where(lane == k, jnp.sum(racc[k], axis=1, keepdims=True), cols)
    return jnp.transpose(cols)[0:8, :]


def rows_of(pack):
    lane = iota((8, 128), 1)
    return jnp.where(lane < 64, pack[0, 32:40, :], pack[1, 32:40, :])


def pairs_two(stars, near, ab, out, token):
    token[...] = jnp.zeros((8, 128), F32)
    spread(rows_of(near), ab)
    pair_loop(stars, ab, None, out)


def pairs_four(got, stars, far, ab_near, near_in, after, ab_far, sums, racc):
    pair_loop(got, ab_near, near_in, racc)
    sums[0] = lane_sums(racc) + after[...]
    spread(rows_of(far), ab_far)
    pair_loop(stars, ab_far, None, racc)
    sums[1] = lane_sums(racc)


def pairs_eight(got, ab_near, ab_far, near_out, far_out):
    pair_loop(got, ab_far, None, far_out)
    pair_loop(got, ab_near, None, near_out)


def irregular(blk, pack, tables):
    row = iota((8, 128), 0)
    z = (row >> 1) ^ (row >> 2)
    shard0 = blk ^ ((z << 1) ^ (row & 1))
    owners = [shard0.astype(F32), (shard0 ^ 32).astype(F32)]
    out = []
    for t in range(2):
        ids = pack[t, 0:32, :]
        owner = jnp.floor(ids * (1.0 / 512.0))
        local = ids - 512.0 * owner
        act = pack[t, 32:40, :]
        own = [jnp.broadcast_to(act[c : c + 1, :], (8, 128)) for c in range(6)]
        zero = jnp.zeros((8, 128), F32)
        owner_rows = [jnp.broadcast_to(owner[k : k + 1, :], (8, 128)) for k in range(32)]
        local_rows = [jnp.broadcast_to(local[k : k + 1, :], (8, 128)) for k in range(32)]

        def scan(layer):
            found = []
            for u in range(2):
                seen, pos = zero, zero
                for k in range(32):
                    hit = owner_rows[k] == owners[u]
                    pos = jnp.where(hit & (seen == layer), local_rows[k], pos)
                    seen = jnp.where(hit, seen + 1.0, seen)
                found.append((seen, pos))
            return found

        def add(layer, acc):
            level = layer.astype(F32)
            acc = list(acc)
            for u, (seen, pos) in enumerate(scan(level)):
                idx = pos.astype(I32)
                part = idx >> 7
                lane = idx & 127
                other = []
                for c in range(7):
                    got = lane_gather(tables[u][:, c, 0:128], lane)
                    for k in range(1, 4):
                        tab = tables[u][:, c, 128 * k : 128 * k + 128]
                        got = jnp.where(part == k, lane_gather(tab, lane), got)
                    other.append(got)
                other[6] = jnp.where(seen > level, other[6], 0.0)
                acc = pair_terms(other, own, acc)
            return tuple(acc)

        most = zero
        for u in range(2):
            seen = zero
            for k in range(32):
                seen = jnp.where(owner_rows[k] == owners[u], seen + 1.0, seen)
            most = jnp.maximum(most, seen)
        layers = jnp.max(most).astype(I32)
        acc = lax.fori_loop(0, layers, add, (zero,) * 9)
        sums = jnp.concatenate([jnp.sum(r, axis=0, keepdims=True) for r in finish(acc)], axis=0)
        out.append(sums + pltpu.roll(sums, 64, 1))
    lane = iota((6, 128), 1)
    return jnp.where(lane < 64, out[0], out[1])


def last_kernel(which, blk, first, second, pack, ab, before, sums, out, racc):
    pair_loop(second, ab, before, racc)
    irr = irregular(blk[0], pack, (first, second))
    out[0:6, :] = (lane_sums(racc) + sums[which])[0:6, :]
    out[6:12, :] = irr
    out[12:16, :] = jnp.zeros((4, 128), F32)


def final_kernel(own, near, got, new, regular, irr):
    lane64 = slice(0, 64)
    every = near[:, lane64] + got[:, 64:128]
    total = every[0:6]
    state = own[:, lane64]
    half = 0.5 * time_step
    twelfth = time_step * time_step / 12.0
    vel = state[3:6] + half * (state[6:9] + total[0:3]) + twelfth * (state[9:12] - total[3:6])
    pos = state[0:3] + half * (state[3:6] + vel) + twelfth * (state[6:9] - total[0:3])
    new[...] = jnp.concatenate([pos, vel], axis=0)
    irr[...] = every[6:12]
    regular[...] = total - every[6:12]


def shape(*dims):
    return jax.ShapeDtypeStruct(dims, F32)


def near_memory(*dims):
    return pltpu.VMEM(dims, F32)


def held(*values):
    return [pltpu.with_memory_space_constraint(v, pltpu.VMEM) for v in values]


def exchange(value, mask):
    return lax.ppermute(value, "blk", [(b, b ^ mask) for b in range(64)])


def per_device(star_state, active_local, neighbours, counts):
    blk = lax.axis_index("blk").astype(I32).reshape(1)
    stars, pack, own = pl.pallas_call(
        prep_kernel,
        out_shape=(near_memory(8, 512), near_memory(40, 128), near_memory(16, 128)),
        name="prep",
    )(star_state, active_local.reshape(1, 64), neighbours, counts.reshape(1, 64))
    stars2 = jnp.stack([stars, exchange(stars, 1)])
    sent = exchange(stars2, 2)
    got_pack, stars2 = lax.optimization_barrier((exchange(pack, 8), stars2))
    near = jnp.stack([pack, got_pack])
    block = near_memory(6, 128, 128)
    small = near_memory(8, 128)
    ab_near, near2, token = pl.pallas_call(
        pairs_two, out_shape=(block, block, small), name="pairs_two"
    )(*held(stars2, near))
    far, got2, token = lax.optimization_barrier((exchange(near, 24), sent, token))
    stars4 = jnp.concatenate([stars2, got2])
    ab_far, sums4 = pl.pallas_call(
        pairs_four,
        out_shape=(block, near_memory(2, 8, 128)),
        scratch_shapes=[pltpu.VMEM((6, 128, 128), F32)],
        name="pairs_four",
    )(*held(got2, stars4, far, ab_near, near2, token))
    got4, sums4 = lax.optimization_barrier((exchange(stars4, 6), sums4))
    stars8 = jnp.concatenate([stars4, got4])
    other8 = exchange(stars8, 32)
    near8, far8 = pl.pallas_call(pairs_eight, out_shape=(block, block), name="pairs_eight")(
        *held(got4, ab_near, ab_far)
    )
    smem = pl.BlockSpec(memory_space=pltpu.SMEM)
    vmem = pl.BlockSpec(memory_space=pltpu.VMEM)

    def last(which, pack, ab, part, name):
        return pl.pallas_call(
            functools.partial(last_kernel, which),
            in_specs=[smem] + [vmem] * 6,
            out_shape=near_memory(16, 128),
            scratch_shapes=[pltpu.VMEM((6, 128, 128), F32)],
            name=name,
        )(blk, *held(stars8, other8, pack, ab, part, sums4))

    far_sum = last(1, far, ab_far, far8, "pairs_far")
    got_far = exchange(far_sum, 24)
    near_sum = last(0, near, ab_near, near8, "pairs_near") + got_far
    got_near = exchange(near_sum, 8)
    return pl.pallas_call(
        final_kernel, out_shape=(shape(6, 64), shape(6, 64), shape(6, 64)), name="final"
    )(*held(own, near_sum, got_near))


def solution(mesh):
    in_specs = (P(None, "blk"), P(("blk", "grp")), P(("blk", "grp"), None), P(("blk", "grp")))
    out_specs = (P(None, ("blk", "grp")), P(None, ("blk", "grp")), P(None, ("blk", "grp")))
    return jax.shard_map(
        per_device, mesh=mesh, in_specs=in_specs, out_specs=out_specs, check_vma=False
    )
```

```python
import functools
import jax
import jax.numpy as jnp
from jax import lax
from jax.experimental import pallas as pl
from jax.experimental.pallas import tpu as pltpu
from jax.sharding import PartitionSpec as P

time_step = 0.0078125
soften_sq = 0.001
F32 = jnp.float32
I32 = jnp.int32


def iota(shape, dim):
    return lax.broadcasted_iota(I32, shape, dim)


def lane_gather(table, lane):
    return jnp.take_along_axis(table, lane, axis=1, mode="promise_in_bounds")


def pair_terms(other, own, acc):
    dx = [other[c] - own[c] for c in range(3)]
    dv = [other[3 + c] - own[3 + c] for c in range(3)]
    dist = dx[0] * dx[0] + dx[1] * dx[1] + (dx[2] * dx[2] + soften_sq)
    inv = lax.rsqrt(dist)
    radial = dx[0] * dv[0] + dx[1] * dv[1] + dx[2] * dv[2]
    inv2 = inv * inv
    w = (other[6] * inv) * inv2
    q = radial * inv2
    for c in range(3):
        wx = w * dx[c]
        acc[c] = acc[c] + wx
        acc[3 + c] = acc[3 + c] + w * dv[c]
        acc[6 + c] = acc[6 + c] + q * wx
    return acc


def finish(acc):
    return list(acc[:3]) + [acc[3 + c] - 3.0 * acc[6 + c] for c in range(3)]


def prep_kernel(state, local, nb, counts, stars, pack, own):
    h = time_step
    x, v, a, j = (state[3 * k : 3 * k + 3, :] for k in range(4))
    pos = x + h * (v + h * (0.5 * a + h * j / 6.0))
    vel = v + h * (a + 0.5 * h * j)
    pred = jnp.concatenate([pos, vel, state[12:13, :], jnp.zeros((1, 512), F32)], axis=0)
    stars[...] = pred
    idx = local[...]
    idx = jnp.broadcast_to(jnp.concatenate([idx, idx], axis=1), (8, 128))
    part = idx >> 7
    lane = idx & 127
    low = state[0:8, :]
    high = jnp.concatenate([state[8:13, :], jnp.zeros((3, 512), F32)], axis=0)

    def pick(rows):
        out = lane_gather(rows[:, 0:128], lane)
        for k in range(1, 4):
            out = jnp.where(part == k, lane_gather(rows[:, 128 * k : 128 * k + 128], lane), out)
        return out

    pack[32:40, :] = pick(pred)
    own[0:8, :] = pick(low)
    own[8:16, :] = pick(high)
    ids = nb[...].astype(F32)
    ids = jnp.concatenate([ids, ids], axis=1)
    ids = jnp.transpose(ids)
    half = iota((32, 128), 1) // 64
    cnt = counts[...]
    cnt = jnp.concatenate([cnt, cnt], axis=1)
    both = jnp.concatenate([ids[0:32, :], ids[32:64, :]], axis=1)
    live = iota((32, 128), 0) + 32 * half < cnt
    pack[0:32, :] = jnp.where(live, both, -1.0)


def spread(rows, ab):
    cols = jnp.transpose(rows)
    for c in range(6):
        ab[c] = jnp.broadcast_to(cols[:, c : c + 1], (128, 128))


def pair_loop(stars, ab, before, out):
    count = stars.shape[0]

    def octets(g, carry):
        at = [pl.ds(pl.multiple_of(g * 16 + 8 * t, 8), 8) for t in range(2)]
        own = [[ab[c, at[t], :] for c in range(6)] for t in range(2)]

        def shard(b, acc):
            acc = list(acc)
            for k in range(4):
                lanes = slice(128 * k, 128 * k + 128)
                other = [jnp.broadcast_to(stars[b, c : c + 1, lanes], (8, 128)) for c in range(7)]
                for t in range(2):
                    acc[9 * t : 9 * t + 9] = pair_terms(other, own[t], acc[9 * t : 9 * t + 9])
            return tuple(acc)

        acc = lax.fori_loop(0, count, shard, (jnp.zeros((8, 128), F32),) * 18)
        for t in range(2):
            for k, val in enumerate(finish(acc[9 * t : 9 * t + 9])):
                out[k, at[t], :] = val if before is None else val + before[k, at[t], :]
        return carry

    lax.fori_loop(0, 8, octets, 0)


def lane_sums(racc):
    lane = iota((128, 128), 1)
    cols = jnp.zeros((128, 128), F32)
    for k in range(6):
        cols = jnp.where(lane == k, jnp.sum(racc[k], axis=1, keepdims=True), cols)
    return jnp.transpose(cols)[0:8, :]


def rows_of(pack):
    lane = iota((8, 128), 1)
    return jnp.where(lane < 64, pack[0, 32:40, :], pack[1, 32:40, :])


def pairs_two(stars, near, ab, out, token):
    token[...] = jnp.zeros((8, 128), F32)
    spread(rows_of(near), ab)
    pair_loop(stars, ab, None, out)


def pairs_more(got, ab_near, near_in, after, sums, racc):
    pair_loop(got, ab_near, near_in, racc)
    sums[...] = lane_sums(racc) + after[...]


def pairs_four(stars, far, after, ab_far, sums, racc):
    sums[0] = after[...]
    spread(rows_of(far), ab_far)
    pair_loop(stars, ab_far, None, racc)
    sums[1] = lane_sums(racc)


def pairs_eight(got, ab_near, ab_far, near_out, far_out):
    pair_loop(got, ab_far, None, far_out)
    pair_loop(got, ab_near, None, near_out)


def irregular(blk, pack, tables):
    row = iota((8, 128), 0)
    z = (row >> 1) ^ (row >> 2)
    shard0 = blk ^ ((z << 1) ^ (row & 1))
    owners = [shard0.astype(F32), (shard0 ^ 32).astype(F32)]
    out = []
    for t in range(2):
        ids = pack[t, 0:32, :]
        owner = jnp.floor(ids * (1.0 / 512.0))
        local = ids - 512.0 * owner
        act = pack[t, 32:40, :]
        own = [jnp.broadcast_to(act[c : c + 1, :], (8, 128)) for c in range(6)]
        zero = jnp.zeros((8, 128), F32)
        owner_rows = [jnp.broadcast_to(owner[k : k + 1, :], (8, 128)) for k in range(32)]
        local_rows = [jnp.broadcast_to(local[k : k + 1, :], (8, 128)) for k in range(32)]

        def scan(layer):
            found = []
            for u in range(2):
                seen, pos = zero, zero
                for k in range(32):
                    hit = owner_rows[k] == owners[u]
                    pos = jnp.where(hit & (seen == layer), local_rows[k], pos)
                    seen = jnp.where(hit, seen + 1.0, seen)
                found.append((seen, pos))
            return found

        def add(layer, acc):
            level = layer.astype(F32)
            acc = list(acc)
            for u, (seen, pos) in enumerate(scan(level)):
                idx = pos.astype(I32)
                part = idx >> 7
                lane = idx & 127
                other = []
                for c in range(7):
                    got = lane_gather(tables[u][:, c, 0:128], lane)
                    for k in range(1, 4):
                        tab = tables[u][:, c, 128 * k : 128 * k + 128]
                        got = jnp.where(part == k, lane_gather(tab, lane), got)
                    other.append(got)
                other[6] = jnp.where(seen > level, other[6], 0.0)
                acc = pair_terms(other, own, acc)
            return tuple(acc)

        most = zero
        for u in range(2):
            seen = zero
            for k in range(32):
                seen = jnp.where(owner_rows[k] == owners[u], seen + 1.0, seen)
            most = jnp.maximum(most, seen)
        layers = jnp.max(most).astype(I32)
        acc = lax.fori_loop(0, layers, add, (zero,) * 9)
        sums = jnp.concatenate([jnp.sum(r, axis=0, keepdims=True) for r in finish(acc)], axis=0)
        out.append(sums + pltpu.roll(sums, 64, 1))
    lane = iota((6, 128), 1)
    return jnp.where(lane < 64, out[0], out[1])


def last_kernel(which, blk, first, second, pack, ab, before, sums, out, racc):
    pair_loop(second, ab, before, racc)
    irr = irregular(blk[0], pack, (first, second))
    out[0:6, :] = (lane_sums(racc) + sums[which])[0:6, :]
    out[6:12, :] = irr
    out[12:16, :] = jnp.zeros((4, 128), F32)


def final_kernel(own, near, got, new, regular, irr):
    lane64 = slice(0, 64)
    every = near[:, lane64] + got[:, 64:128]
    total = every[0:6]
    state = own[:, lane64]
    half = 0.5 * time_step
    twelfth = time_step * time_step / 12.0
    vel = state[3:6] + half * (state[6:9] + total[0:3]) + twelfth * (state[9:12] - total[3:6])
    pos = state[0:3] + half * (state[3:6] + vel) + twelfth * (state[6:9] - total[0:3])
    new[...] = jnp.concatenate([pos, vel], axis=0)
    irr[...] = every[6:12]
    regular[...] = total - every[6:12]


def shape(*dims):
    return jax.ShapeDtypeStruct(dims, F32)


def near_memory(*dims):
    return pltpu.VMEM(dims, F32)


def held(*values):
    return [pltpu.with_memory_space_constraint(v, pltpu.VMEM) for v in values]


def exchange(value, mask):
    return lax.ppermute(value, "blk", [(b, b ^ mask) for b in range(64)])


def per_device(star_state, active_local, neighbours, counts):
    blk = lax.axis_index("blk").astype(I32).reshape(1)
    stars, pack, own = pl.pallas_call(
        prep_kernel,
        out_shape=(near_memory(8, 512), near_memory(40, 128), near_memory(16, 128)),
        name="prep",
    )(star_state, active_local.reshape(1, 64), neighbours, counts.reshape(1, 64))
    stars2 = jnp.stack([stars, exchange(stars, 1)])
    sent = exchange(stars2, 2)
    got_pack, stars2 = lax.optimization_barrier((exchange(pack, 8), stars2))
    near = jnp.stack([pack, got_pack])
    block = near_memory(6, 128, 128)
    small = near_memory(8, 128)
    ab_near, near2, token = pl.pallas_call(
        pairs_two, out_shape=(block, block, small), name="pairs_two"
    )(*held(stars2, near))
    far = exchange(near, 24)
    got2, token = lax.optimization_barrier((sent, token))
    stars4 = jnp.concatenate([stars2, got2])
    got4 = exchange(stars4, 6)
    scratch = [pltpu.VMEM((6, 128, 128), F32)]
    token = pl.pallas_call(pairs_more, out_shape=small, scratch_shapes=scratch, name="pairs_more")(
        *held(got2, ab_near, near2, token)
    )
    far, token = lax.optimization_barrier((far, token))
    ab_far, sums4 = pl.pallas_call(
        pairs_four,
        out_shape=(block, near_memory(2, 8, 128)),
        scratch_shapes=scratch,
        name="pairs_four",
    )(*held(stars4, far, token))
    got4, sums4 = lax.optimization_barrier((got4, sums4))
    stars8 = jnp.concatenate([stars4, got4])
    other8 = exchange(stars8, 32)
    near8, far8 = pl.pallas_call(pairs_eight, out_shape=(block, block), name="pairs_eight")(
        *held(got4, ab_near, ab_far)
    )
    smem = pl.BlockSpec(memory_space=pltpu.SMEM)
    vmem = pl.BlockSpec(memory_space=pltpu.VMEM)

    def last(which, pack, ab, part, name):
        return pl.pallas_call(
            functools.partial(last_kernel, which),
            in_specs=[smem] + [vmem] * 6,
            out_shape=near_memory(16, 128),
            scratch_shapes=[pltpu.VMEM((6, 128, 128), F32)],
            name=name,
        )(blk, *held(stars8, other8, pack, ab, part, sums4))

    far_sum = last(1, far, ab_far, far8, "pairs_far")
    got_far = exchange(far_sum, 24)
    near_sum = last(0, near, ab_near, near8, "pairs_near") + got_far
    got_near = exchange(near_sum, 8)
    return pl.pallas_call(
        final_kernel, out_shape=(shape(6, 64), shape(6, 64), shape(6, 64)), name="final"
    )(*held(own, near_sum, got_near))


def solution(mesh):
    in_specs = (P(None, "blk"), P(("blk", "grp")), P(("blk", "grp"), None), P(("blk", "grp")))
    out_specs = (P(None, ("blk", "grp")), P(None, ("blk", "grp")), P(None, ("blk", "grp")))
    return jax.shard_map(
        per_device, mesh=mesh, in_specs=in_specs, out_specs=out_specs, check_vma=False
    )
```

```python
import functools
import jax
import jax.numpy as jnp
from jax import lax
from jax.experimental import pallas as pl
from jax.experimental.pallas import tpu as pltpu
from jax.sharding import PartitionSpec as P

time_step = 0.0078125
soften_sq = 0.001
F32 = jnp.float32
I32 = jnp.int32


def iota(shape, dim):
    return lax.broadcasted_iota(I32, shape, dim)


def lane_gather(table, lane):
    return jnp.take_along_axis(table, lane, axis=1, mode="promise_in_bounds")


def pair_terms(other, own, acc):
    dx = [other[c] - own[c] for c in range(3)]
    dv = [other[3 + c] - own[3 + c] for c in range(3)]
    dist = dx[0] * dx[0] + dx[1] * dx[1] + (dx[2] * dx[2] + soften_sq)
    inv = lax.rsqrt(dist)
    radial = dx[0] * dv[0] + dx[1] * dv[1] + dx[2] * dv[2]
    inv2 = inv * inv
    w = (other[6] * inv) * inv2
    q = radial * inv2
    for c in range(3):
        wx = w * dx[c]
        acc[c] = acc[c] + wx
        acc[3 + c] = acc[3 + c] + w * dv[c]
        acc[6 + c] = acc[6 + c] + q * wx
    return acc


def finish(acc):
    return list(acc[:3]) + [acc[3 + c] - 3.0 * acc[6 + c] for c in range(3)]


def prep_kernel(state, local, nb, counts, stars, pack, own):
    h = time_step
    x, v, a, j = (state[3 * k : 3 * k + 3, :] for k in range(4))
    pos = x + h * (v + h * (0.5 * a + h * j / 6.0))
    vel = v + h * (a + 0.5 * h * j)
    pred = jnp.concatenate([pos, vel, state[12:13, :], jnp.zeros((1, 512), F32)], axis=0)
    stars[...] = pred
    idx = local[...]
    idx = jnp.broadcast_to(jnp.concatenate([idx, idx], axis=1), (8, 128))
    part = idx >> 7
    lane = idx & 127
    low = state[0:8, :]
    high = jnp.concatenate([state[8:13, :], jnp.zeros((3, 512), F32)], axis=0)

    def pick(rows):
        out = lane_gather(rows[:, 0:128], lane)
        for k in range(1, 4):
            out = jnp.where(part == k, lane_gather(rows[:, 128 * k : 128 * k + 128], lane), out)
        return out

    pack[32:40, :] = pick(pred)
    own[0:8, :] = pick(low)
    own[8:16, :] = pick(high)
    ids = nb[...].astype(F32)
    ids = jnp.concatenate([ids, ids], axis=1)
    ids = jnp.transpose(ids)
    half = iota((32, 128), 1) // 64
    cnt = counts[...]
    cnt = jnp.concatenate([cnt, cnt], axis=1)
    both = jnp.concatenate([ids[0:32, :], ids[32:64, :]], axis=1)
    live = iota((32, 128), 0) + 32 * half < cnt
    pack[0:32, :] = jnp.where(live, both, -1.0)


def spread(rows, ab):
    cols = jnp.transpose(rows)
    for c in range(6):
        ab[c] = jnp.broadcast_to(cols[:, c : c + 1], (128, 128))


def pair_loop(stars, ab, before, out):
    count = stars.shape[0]

    def octets(g, carry):
        at = [pl.ds(pl.multiple_of(g * 16 + 8 * t, 8), 8) for t in range(2)]
        own = [[ab[c, at[t], :] for c in range(6)] for t in range(2)]

        def shard(b, acc):
            acc = list(acc)
            for k in range(4):
                lanes = slice(128 * k, 128 * k + 128)
                other = [jnp.broadcast_to(stars[b, c : c + 1, lanes], (8, 128)) for c in range(7)]
                for t in range(2):
                    acc[9 * t : 9 * t + 9] = pair_terms(other, own[t], acc[9 * t : 9 * t + 9])
            return tuple(acc)

        acc = lax.fori_loop(0, count, shard, (jnp.zeros((8, 128), F32),) * 18, unroll=2)
        for t in range(2):
            for k, val in enumerate(finish(acc[9 * t : 9 * t + 9])):
                out[k, at[t], :] = val if before is None else val + before[k, at[t], :]
        return carry

    lax.fori_loop(0, 8, octets, 0)


def lane_sums(racc):
    lane = iota((128, 128), 1)
    cols = jnp.zeros((128, 128), F32)
    for k in range(6):
        cols = jnp.where(lane == k, jnp.sum(racc[k], axis=1, keepdims=True), cols)
    return jnp.transpose(cols)[0:8, :]


def rows_of(pack):
    lane = iota((8, 128), 1)
    return jnp.where(lane < 64, pack[0, 32:40, :], pack[1, 32:40, :])


def pairs_two(stars, near, ab, out, token):
    token[...] = jnp.zeros((8, 128), F32)
    spread(rows_of(near), ab)
    pair_loop(stars, ab, None, out)


def pairs_four(got, stars, far, ab_near, near_in, after, ab_far, sums, racc):
    pair_loop(got, ab_near, near_in, racc)
    sums[0] = lane_sums(racc) + after[...]
    spread(rows_of(far), ab_far)
    pair_loop(stars, ab_far, None, racc)
    sums[1] = lane_sums(racc)


def pairs_eight(got, ab_near, ab_far, near_out, far_out):
    pair_loop(got, ab_far, None, far_out)
    pair_loop(got, ab_near, None, near_out)


def irregular(blk, pack, tables):
    row = iota((8, 128), 0)
    z = (row >> 1) ^ (row >> 2)
    shard0 = blk ^ ((z << 1) ^ (row & 1))
    owners = [shard0.astype(F32), (shard0 ^ 32).astype(F32)]
    out = []
    for t in range(2):
        ids = pack[t, 0:32, :]
        owner = jnp.floor(ids * (1.0 / 512.0))
        local = ids - 512.0 * owner
        act = pack[t, 32:40, :]
        own = [jnp.broadcast_to(act[c : c + 1, :], (8, 128)) for c in range(6)]
        zero = jnp.zeros((8, 128), F32)
        owner_rows = [jnp.broadcast_to(owner[k : k + 1, :], (8, 128)) for k in range(32)]
        local_rows = [jnp.broadcast_to(local[k : k + 1, :], (8, 128)) for k in range(32)]

        def scan(layer):
            found = []
            for u in range(2):
                seen, pos = zero, zero
                for k in range(32):
                    hit = owner_rows[k] == owners[u]
                    pos = jnp.where(hit & (seen == layer), local_rows[k], pos)
                    seen = jnp.where(hit, seen + 1.0, seen)
                found.append((seen, pos))
            return found

        def add(layer, acc):
            level = layer.astype(F32)
            acc = list(acc)
            for u, (seen, pos) in enumerate(scan(level)):
                idx = pos.astype(I32)
                part = idx >> 7
                lane = idx & 127
                other = []
                for c in range(7):
                    got = lane_gather(tables[u][:, c, 0:128], lane)
                    for k in range(1, 4):
                        tab = tables[u][:, c, 128 * k : 128 * k + 128]
                        got = jnp.where(part == k, lane_gather(tab, lane), got)
                    other.append(got)
                other[6] = jnp.where(seen > level, other[6], 0.0)
                acc = pair_terms(other, own, acc)
            return tuple(acc)

        most = zero
        for u in range(2):
            seen = zero
            for k in range(32):
                seen = jnp.where(owner_rows[k] == owners[u], seen + 1.0, seen)
            most = jnp.maximum(most, seen)
        layers = jnp.max(most).astype(I32)
        acc = lax.fori_loop(0, layers, add, (zero,) * 9)
        sums = jnp.concatenate([jnp.sum(r, axis=0, keepdims=True) for r in finish(acc)], axis=0)
        out.append(sums + pltpu.roll(sums, 64, 1))
    lane = iota((6, 128), 1)
    return jnp.where(lane < 64, out[0], out[1])


def last_kernel(which, blk, first, second, pack, ab, before, sums, out, racc):
    pair_loop(second, ab, before, racc)
    irr = irregular(blk[0], pack, (first, second))
    out[0:6, :] = (lane_sums(racc) + sums[which])[0:6, :]
    out[6:12, :] = irr
    out[12:16, :] = jnp.zeros((4, 128), F32)


def final_kernel(own, near, got, new, regular, irr):
    lane64 = slice(0, 64)
    every = near[:, lane64] + got[:, 64:128]
    total = every[0:6]
    state = own[:, lane64]
    half = 0.5 * time_step
    twelfth = time_step * time_step / 12.0
    vel = state[3:6] + half * (state[6:9] + total[0:3]) + twelfth * (state[9:12] - total[3:6])
    pos = state[0:3] + half * (state[3:6] + vel) + twelfth * (state[6:9] - total[0:3])
    new[...] = jnp.concatenate([pos, vel], axis=0)
    irr[...] = every[6:12]
    regular[...] = total - every[6:12]


def shape(*dims):
    return jax.ShapeDtypeStruct(dims, F32)


def near_memory(*dims):
    return pltpu.VMEM(dims, F32)


def held(*values):
    return [pltpu.with_memory_space_constraint(v, pltpu.VMEM) for v in values]


def exchange(value, mask):
    return lax.ppermute(value, "blk", [(b, b ^ mask) for b in range(64)])


def per_device(star_state, active_local, neighbours, counts):
    blk = lax.axis_index("blk").astype(I32).reshape(1)
    stars, pack, own = pl.pallas_call(
        prep_kernel,
        out_shape=(near_memory(8, 512), near_memory(40, 128), near_memory(16, 128)),
        name="prep",
    )(star_state, active_local.reshape(1, 64), neighbours, counts.reshape(1, 64))
    got = lax.optimization_barrier((exchange(stars, 1), exchange(pack, 8)))
    stars2 = jnp.stack([stars, got[0]])
    near = jnp.stack([pack, got[1]])
    block = near_memory(6, 128, 128)
    small = near_memory(8, 128)
    ab_near, near2, token = pl.pallas_call(
        pairs_two, out_shape=(block, block, small), name="pairs_two"
    )(*held(stars2, near))
    far, got2, token = lax.optimization_barrier((exchange(near, 24), exchange(stars2, 2), token))
    stars4 = jnp.concatenate([stars2, got2])
    ab_far, sums4 = pl.pallas_call(
        pairs_four,
        out_shape=(block, near_memory(2, 8, 128)),
        scratch_shapes=[pltpu.VMEM((6, 128, 128), F32)],
        name="pairs_four",
    )(*held(got2, stars4, far, ab_near, near2, token))
    got4, sums4 = lax.optimization_barrier((exchange(stars4, 6), sums4))
    stars8 = jnp.concatenate([stars4, got4])
    other8 = exchange(stars8, 32)
    near8, far8 = pl.pallas_call(pairs_eight, out_shape=(block, block), name="pairs_eight")(
        *held(got4, ab_near, ab_far)
    )
    smem = pl.BlockSpec(memory_space=pltpu.SMEM)
    vmem = pl.BlockSpec(memory_space=pltpu.VMEM)

    def last(which, pack, ab, part, name):
        return pl.pallas_call(
            functools.partial(last_kernel, which),
            in_specs=[smem] + [vmem] * 6,
            out_shape=near_memory(16, 128),
            scratch_shapes=[pltpu.VMEM((6, 128, 128), F32)],
            name=name,
        )(blk, *held(stars8, other8, pack, ab, part, sums4))

    far_sum = last(1, far, ab_far, far8, "pairs_far")
    got_far = exchange(far_sum, 24)
    near_sum = last(0, near, ab_near, near8, "pairs_near") + got_far
    got_near = exchange(near_sum, 8)
    return pl.pallas_call(
        final_kernel, out_shape=(shape(6, 64), shape(6, 64), shape(6, 64)), name="final"
    )(*held(own, near_sum, got_near))


def solution(mesh):
    in_specs = (P(None, "blk"), P(("blk", "grp")), P(("blk", "grp"), None), P(("blk", "grp")))
    out_specs = (P(None, ("blk", "grp")), P(None, ("blk", "grp")), P(None, ("blk", "grp")))
    return jax.shard_map(
        per_device, mesh=mesh, in_specs=in_specs, out_specs=out_specs, check_vma=False
    )
```
